32 devices in a mesh: groups: 2 (over y), seq: 4 (over z), head: 4 (over x, core).
Axes of the slice: x: 2, y: 2, z: 4, core: 2. Of those that a mesh axis runs over, the one named last changes fastest.
Arguments:
- query_latent_rows: bfloat16 [640, 1536], P(('groups', 'seq')), parts along dimension 0, may hold values from -6 to 6
- key_value_latents: bfloat16 [640, 576], P(('groups', 'seq')), parts along dimension 0, may hold values from -500 to 500
- positions: int32 [640], P(('groups', 'seq')), parts along dimension 0, may hold values from 130752 to 131071, as said below
- query_up_weight: bfloat16 [1536, 12288], P('seq', 'head'), may hold values from -0.15625 to 0.15625
- adapter_down_factor: bfloat16 [3072, 64], P(('groups', 'seq')), parts along dimension 0, may hold values from -0.75 to 0.75
- adapter_up_factor: bfloat16 [128, 12288], P('groups', 'head'), parts along dimension 0, may hold values from -0.15625 to 0.15625
- head_key_up_weight: bfloat16 [64, 128, 512], P('head'), may hold values from -0.5 to 0.5
- head_value_up_weight: bfloat16 [64, 512, 128], P('head'), may hold values from -0.25 to 0.25
- output_projection_weight: bfloat16 [8192, 7168], P('head', 'seq'), may hold values from -0.0625 to 0.0625
Outputs:
- merged_weight: bfloat16 [3072, 12288], P(('groups', 'seq'), 'head'), parts along dimension 0
- mixed: bfloat16 [640, 7168], P(('groups', 'head'), 'seq'), parts along dimension 0
The draws below stay inside these ranges and needn't reach their ends.
There are 2 independent parts, one for each index of `groups`. The reference program is written for one: setup_inputs(seed, part) draws one part's arguments, and reference() takes and returns one part's arrays. A program takes and returns all parts, laid end to end along the dimension named above; an argument that names none is the same for every part. Nothing has to cross between parts.
Inputs may be any that keep to these rules, and one draw needn't show every extreme that they name: positions are distinct; each aligned block of 80 rows holds 80 consecutive positions in rising order, and the blocks together cover the last 320 positions of the prompt in an order drawn from the seed.
All inputs are finite; a program needn't handle non-finite values.
Results may differ from the reference program's by a relative error of at most 0.015.
The reference program's roundings to bfloat16 on the way count: a program that leaves them out, or rounds other values in their place, can miss the bound.
Values may be sent and summed in bfloat16 or wider, within the bound.
A program may use at most 64 MiB of HBM per device.

```python
import math
import jax
import jax.numpy as jnp
from jax import lax

QUERY_LATENT = 1536
HEADS = 64
NOPE = 128
ROPE = 64
KVR = 512
VDIM = 128
D = 7168
ADAPTER_RANK = 64
TOK_DEV = 80
TOKENS = 320
QUERY_UP_COLUMNS = 12288


def draw_positions(key, part):
    order = jax.random.permutation(jax.random.fold_in(key, 11), TOKENS // TOK_DEV)
    begin = 131072 - TOKENS
    index = jnp.arange(TOKENS, dtype=jnp.int32)
    inner = index % TOK_DEV
    block = index // TOK_DEV
    return (begin + order[block] * TOK_DEV + inner).astype(jnp.int32)


def draw_key_value_latents(key, part):
    base = jax.random.normal(jax.random.fold_in(key, 21), (TOKENS, KVR + ROPE), jnp.float32)
    return base.astype(jnp.bfloat16)


def block_levels(own_key, shape, pieces, smallest, largest):
    def one(dim, parts):
        steps = jax.random.uniform(jax.random.fold_in(jax.random.fold_in(own_key, 6), dim), (parts,), jnp.float32, smallest / len(pieces), largest / len(pieces))
        return jnp.repeat(jnp.exp(steps), shape[dim] // parts).reshape((-1,) + (1,) * (len(shape) - dim - 1))

    level = one(*pieces[0])
    for cut in pieces[1:]:
        level = level * one(*cut)
    return level


def bell_draw(stream_key, extent, deviation, reach, cuts=(), kind=jnp.bfloat16):
    values = deviation * jax.random.normal(stream_key, extent, jnp.float32)
    if cuts:
        values = values * block_levels(stream_key, extent, cuts, -0.22, 0.18)
    return jnp.clip(values, -reach, reach).astype(kind)


def setup_inputs(seed: int = 0, part: int = 0) -> dict:
    seeds = jax.random.split(jax.random.key(seed), 10)
    part_keys = jax.random.split(jax.random.fold_in(seeds[9], part), 10)
    query_latent_rows = bell_draw(part_keys[0], (TOKENS, QUERY_LATENT), 1.0, 6.0, ((0, 4),))
    key_value_latents = draw_key_value_latents(jax.random.fold_in(jax.random.fold_in(seeds[9], part), 71), part)
    positions = draw_positions(jax.random.fold_in(jax.random.fold_in(seeds[9], part), 71), part)
    query_up_weight = bell_draw(seeds[3], (QUERY_LATENT, QUERY_UP_COLUMNS), QUERY_LATENT ** -0.5, 0.15625, ((0, 4), (1, 4)))
    adapter_down_factor = bell_draw(part_keys[4], (QUERY_LATENT, ADAPTER_RANK), ADAPTER_RANK ** -0.5, 0.75, ((0, 4),))
    adapter_up_factor = bell_draw(part_keys[5], (ADAPTER_RANK, QUERY_UP_COLUMNS), QUERY_LATENT ** -0.5, 0.15625, ((1, 4),))
    head_key_up_weight = bell_draw(seeds[6], (HEADS, NOPE, KVR), NOPE ** -0.5, 0.5, ((0, 4),))
    head_value_up_weight = bell_draw(seeds[7], (HEADS, KVR, VDIM), KVR ** -0.5, 0.25, ((0, 4),))
    output_projection_weight = bell_draw(seeds[8], (HEADS * VDIM, D), (HEADS * VDIM) ** -0.5, 0.0625, ((0, 4), (1, 4)))
    return dict(query_latent_rows=query_latent_rows, key_value_latents=key_value_latents, positions=positions, query_up_weight=query_up_weight, adapter_down_factor=adapter_down_factor, adapter_up_factor=adapter_up_factor, head_key_up_weight=head_key_up_weight, head_value_up_weight=head_value_up_weight, output_projection_weight=output_projection_weight)


def reference(query_latent_rows, key_value_latents, positions, query_up_weight, adapter_down_factor, adapter_up_factor, head_key_up_weight, head_value_up_weight, output_projection_weight):
    merged_query_weight = (query_up_weight.astype(jnp.float32) + jnp.dot(adapter_down_factor, adapter_up_factor, preferred_element_type=jnp.float32)).astype(jnp.bfloat16)
    queries = jnp.dot(query_latent_rows, merged_query_weight, preferred_element_type=jnp.float32).astype(jnp.bfloat16)
    queries = queries.reshape(TOKENS, HEADS, NOPE + ROPE)
    absorbed = jnp.einsum('thn,hnk->thk', queries[:, :, :NOPE].astype(jnp.float32), head_key_up_weight.astype(jnp.float32)).astype(jnp.bfloat16)
    full_query = jnp.concatenate([absorbed, queries[:, :, NOPE:]], axis=2)
    visible = positions[None, :] <= positions[:, None]
    values = key_value_latents[:, :KVR]
    score_scale = 1.0 / math.sqrt(NOPE + ROPE)

    def one_head(inputs):
        head_query, head_value = inputs
        scores = jnp.dot(head_query, key_value_latents.T, preferred_element_type=jnp.float32) * score_scale
        scores = jnp.where(visible, scores, jnp.float32(-1e+30))
        row_max = lax.optimization_barrier(jnp.max(scores, axis=1, keepdims=True))
        weights = jnp.where(visible, jnp.exp(scores - row_max), jnp.float32(0.0))
        row_sum = lax.optimization_barrier(jnp.sum(weights, axis=1))
        context_output = jnp.dot(weights.astype(jnp.bfloat16), values, preferred_element_type=jnp.float32) / row_sum[:, None]
        context_output = context_output.astype(jnp.bfloat16)
        return jnp.dot(context_output, head_value, preferred_element_type=jnp.float32).astype(jnp.bfloat16)
    per_head = lax.map(one_head, (jnp.transpose(full_query, (1, 0, 2)), head_value_up_weight))
    flattened = jnp.transpose(per_head, (1, 0, 2)).reshape(TOKENS, HEADS * VDIM)
    mixed = jnp.dot(flattened, output_projection_weight, preferred_element_type=jnp.float32).astype(jnp.bfloat16)
    return (merged_query_weight, mixed)
```

```python
import functools
import math

import jax
import jax.numpy as jnp
from jax import lax
from jax.experimental import pallas as pl
from jax.experimental.pallas import tpu as pltpu
from jax.sharding import PartitionSpec as P


MESH = pl.DeviceIdType.MESH


def fused_kernel(dims, w, xk, a, pos, b, key_up, value_up, out_proj, merged, mixed,
                 w_v, a_v, b_v, m_v, xk_all, a_all, pos_all, w_all, mm, ku_v, vu_v, op_v, heads, total,
                 part, got, loc, sx, rx, sy, ry, sa, ra, sb, rb, sp, rp, sw, rw, sv, rv, sh, rh, so, ro):
    S, H, C, T, KQ, NC, nope, rope, kvr, hp, cw, dcols, scale = dims
    qw = nope + rope
    half_k = KQ // 2
    half_x = xk.shape[1] // 2
    ql = S * KQ
    pw = (cw // qw) * (out_proj.shape[0] // (hp * S))
    heads_c = cw // qw
    vdim = out_proj.shape[0] // (hp * S)
    s = lax.axis_index("seq")
    g = lax.axis_index("groups")
    h = lax.axis_index("head")
    other = 1 - g
    core = lax.rem(h, 2)
    sibling = h + 1 - 2 * core

    barrier = pltpu.get_barrier_semaphore()
    for k in range(1, S):
        pl.semaphore_signal(barrier, inc=1, device_id={"seq": lax.rem(s + k, S)}, device_id_type=MESH)
    for k in range(1, H):
        pl.semaphore_signal(barrier, inc=1, device_id={"head": lax.rem(h + k, H)}, device_id_type=MESH)
    pl.semaphore_signal(barrier, inc=1, device_id={"groups": other}, device_id_type=MESH)
    pl.semaphore_wait(barrier, S + H - 1)

    def remote(src, dst, ss, rs, **dev):
        return pltpu.make_async_remote_copy(
            src_ref=src, dst_ref=dst, send_sem=ss, recv_sem=rs, device_id=dev, device_id_type=MESH)

    sends = []

    def go(c):
        c.start()
        sends.append(c)
        return c

    def rows(i):
        return pl.ds(pl.multiple_of(i * T, T), T)

    def xcols(i):
        return pl.ds(pl.multiple_of(i * half_x, 128), half_x)

    def krows(i):
        return pl.ds(pl.multiple_of(i * half_k, 16), half_k)

    gx, ga, gp = {}, {}, {}
    for k in range(1, S):
        p = lax.rem(s + k, S)
        gp[k] = go(remote(pos, pos_all.at[s], sp.at[k], rp.at[k], seq=p))
        ga[k] = go(remote(a.at[krows(core)], a_all.at[s, krows(core)], sa.at[k], ra.at[k], seq=p))
        gx[k] = go(remote(xk.at[:, xcols(core)], xk_all.at[rows(s), xcols(core)], sx.at[k], rx.at[k], seq=p))
    gw = {}

    def wcols(p, c):
        return pl.ds(pl.multiple_of(p * (cw * C) + c * cw, 128), cw)

    for c in range(C):
        for k in range(1, S):
            p = lax.rem(s + k, S)
            gw[c, k] = go(remote(
                w.at[krows(g), wcols(p, c)], w_all.at[c, s, krows(g)], sw.at[c, k], rw.at[c, k], seq=p))
    local = []

    def fetch(src, dst):
        cp = pltpu.make_async_copy(src, dst, loc.at[len(local)])
        cp.start()
        local.append(cp)
        return cp

    first = [fetch(w, w_v), fetch(a, a_v), fetch(b, b_v)]
    own = [fetch(xk, xk_all.at[rows(s)]), fetch(a, a_all.at[s]), fetch(pos, pos_all.at[s])]
    own += [fetch(w.at[:, wcols(s, c)], w_all.at[c, s]) for c in range(C)]
    wts = [fetch(key_up.at[pl.ds(s * hp, hp)], ku_v), fetch(value_up.at[pl.ds(s * hp, hp)], vu_v)]
    ops = []
    for c in range(C):
        for i in range(S):
            ops.append(fetch(out_proj.at[pl.ds((i * hp + c * heads_c) * vdim, pw)], op_v.at[c, pl.ds(i * pw, pw)]))
    for cp in first:
        cp.wait()

    def merge_cols(i, carry):
        cols = pl.ds(pl.multiple_of(i * cw, 128), cw)
        m_v[:, cols] = (w_v[:, cols].astype(jnp.float32) + jnp.dot(
            a_v[...], b_v[:, cols], preferred_element_type=jnp.float32)).astype(jnp.bfloat16)
        return carry

    lax.fori_loop(0, NC // cw, merge_cols, 0)

    yx, ya = {}, {}
    for k in range(1, S):
        q = lax.rem(s - k + S, S)
        ga[k].wait_recv()
        ya[k] = go(remote(a_all.at[q, krows(core)], a_all.at[q, krows(core)], sb.at[k], rb.at[k], head=sibling))
        gx[k].wait_recv()
        yx[k] = go(remote(xk_all.at[rows(q), xcols(core)], xk_all.at[rows(q), xcols(core)], sy.at[k], ry.at[k], head=sibling))
    out_m = pltpu.make_async_copy(m_v, merged, loc.at[len(local)])
    out_m.start()

    def forward(c):
        res = {}
        for k in range(1, S):
            q = lax.rem(s - k + S, S)
            gw[c, k].wait_recv()
            res[k] = go(remote(w_all.at[c, q, krows(g)], w_all.at[c, q, krows(g)], sv.at[c, k], rv.at[c, k], groups=other))
        return res

    q_iota = lax.broadcasted_iota(jnp.int32, (S * T, 1), 0)
    k_iota = lax.broadcasted_iota(jnp.int32, (1, S * T), 1)

    def attend(c):
        for i in range(S):
            mm[i * KQ:(i + 1) * KQ] = (w_all[c, i].astype(jnp.float32) + jnp.dot(
                a_all[i], b_v[:, wcols(s, c)], preferred_element_type=jnp.float32)).astype(jnp.bfloat16)
        queries = jnp.dot(xk_all[:, :ql], mm[...], preferred_element_type=jnp.float32)
        qpos = q_iota
        kpos = k_iota
        for i in range(S):
            start = pos_all[i, 0:1, 0:1] - i * T
            qpos = qpos + jnp.where(q_iota // T == i, start, 0)
            kpos = kpos + jnp.where(k_iota // T == i, start, 0)
        visible = kpos <= qpos
        lat = xk_all[:, ql:ql + kvr]
        key_rope = xk_all[:, ql + kvr:ql + kvr + rope]
        contract = (((1,), (1,)), ((), ()))
        for j in range(heads_c):
            qn = queries[:, j * qw:j * qw + nope].astype(jnp.bfloat16)
            qr = queries[:, j * qw + nope:(j + 1) * qw].astype(jnp.bfloat16)
            absorbed = jnp.dot(qn, ku_v[c * heads_c + j], preferred_element_type=jnp.float32).astype(jnp.bfloat16)
            scores = (lax.dot_general(absorbed, lat, contract, preferred_element_type=jnp.float32)
                      + lax.dot_general(qr, key_rope, contract, preferred_element_type=jnp.float32)) * scale
            scores = jnp.where(visible, scores, jnp.float32(-1e30))
            top = jnp.max(scores, axis=1, keepdims=True)
            weights = jnp.where(visible, jnp.exp(scores - top), jnp.float32(0.0))
            row_sum = jnp.sum(weights, axis=1, keepdims=True)
            context = jnp.dot(weights.astype(jnp.bfloat16), lat, preferred_element_type=jnp.float32)
            context = (context / row_sum).astype(jnp.bfloat16)
            res = jnp.dot(context, vu_v[c * heads_c + j], preferred_element_type=jnp.float32).astype(jnp.bfloat16)
            heads[c, :, pl.ds(pl.multiple_of(s * pw + j * vdim, 128), vdim)] = res
        res = {}
        mine = pl.ds(pl.multiple_of(s * pw, 128), pw)
        for k in range(1, S):
            res[k] = go(remote(heads.at[c, :, mine], heads.at[c, :, mine], sh.at[c, k], rh.at[c, k], seq=lax.rem(s + k, S)))
        return res

    gh = {}
    for c in range(C):
        gv = forward(c)
        if c == 0:
            for cp in own + wts:
                cp.wait()
            for k in range(1, S):
                gp[k].wait_recv()
                ya[k].wait_recv()
                yx[k].wait_recv()
        for k in range(1, S):
            gv[k].wait_recv()
        gh[c] = attend(c)
    for cp in ops:
        cp.wait()
    nb = 2
    bw = dcols // nb
    go_out = {}
    for c in range(C):
        for k in range(1, S):
            gh[c][k].wait_recv()
        for i in range(nb):
            cols = slice(i * bw, (i + 1) * bw)
            acc = jnp.dot(heads[c], op_v[c, :, cols], preferred_element_type=jnp.float32)
            if c > 0:
                acc = acc + total[:, cols]
            if c < C - 1:
                total[:, cols] = acc
            else:
                part[i] = acc.astype(jnp.bfloat16)
                for k in range(1, H):
                    p = lax.rem(h + k, H)
                    go_out[i, k] = go(remote(
                        part.at[i, pl.ds(pl.multiple_of(p * T, T), T)], got.at[i, k], so.at[i, k], ro.at[i, k], head=p))
    for i in range(nb):
        res = part[i, pl.ds(pl.multiple_of(h * T, T), T)].astype(jnp.float32)
        for k in range(1, H):
            go_out[i, k].wait_recv()
            res = res + got[i, k].astype(jnp.float32)
        mixed[:, i * bw:(i + 1) * bw] = res.astype(jnp.bfloat16)
    for cp in sends:
        cp.wait_send()
    out_m.wait()


def fused(mesh_shape, x, kv, positions, w, a, b, key_up, value_up, out_proj):
    S, H = mesh_shape["seq"], mesh_shape["head"]
    T, ql = x.shape
    KQ, NC = w.shape
    hd, nope, kvr = key_up.shape
    rope = kv.shape[1] - kvr
    vdim = value_up.shape[2]
    hp = hd // S
    heads_c = 2
    C = hp // heads_c
    cw = heads_c * (nope + rope)
    dcols = out_proj.shape[1]
    width = ql + kv.shape[1]
    full = -(-width // 256) * 256
    xk = jnp.concatenate([x, kv, jnp.zeros((T, full - width), x.dtype)], axis=1)
    pos = jnp.broadcast_to(positions[:1].reshape(1, 1), (8, 128))
    scale = 1.0 / math.sqrt(nope + rope)
    dims = (S, H, C, T, KQ, NC, nope, rope, kvr, hp, cw, dcols, scale)
    bf, f32 = jnp.bfloat16, jnp.float32
    dma = pltpu.SemaphoreType.DMA
    nloc = 3 + 3 + C + 2 + C * S + 1
    pw = heads_c * vdim
    return pl.pallas_call(
        functools.partial(fused_kernel, dims),
        out_shape=(jax.ShapeDtypeStruct((KQ, NC), bf), jax.ShapeDtypeStruct((T, dcols), bf)),
        in_specs=[pl.BlockSpec(memory_space=pl.ANY)] * 8,
        out_specs=(pl.BlockSpec(memory_space=pl.ANY), pl.BlockSpec(memory_space=pltpu.VMEM)),
        scratch_shapes=[
            pltpu.VMEM((KQ, NC), bf), pltpu.VMEM(a.shape, bf), pltpu.VMEM(b.shape, bf), pltpu.VMEM((KQ, NC), bf),
            pltpu.VMEM((S * T, full), bf), pltpu.VMEM((S,) + a.shape, bf), pltpu.VMEM((S, 8, 128), jnp.int32),
            pltpu.VMEM((C, S, KQ, cw), bf), pltpu.VMEM((S * KQ, cw), bf),
            pltpu.VMEM((hp, nope, kvr), bf), pltpu.VMEM((hp, kvr, vdim), bf),
            pltpu.VMEM((C, S * pw, dcols), bf), pltpu.VMEM((C, S * T, S * pw), bf), pltpu.VMEM((S * T, dcols), f32),
            pltpu.VMEM((2, S * T, dcols // 2), bf), pltpu.VMEM((2, H, T, dcols // 2), bf),
            dma((nloc,)),
            dma((S,)), dma((S,)), dma((S,)), dma((S,)), dma((S,)), dma((S,)), dma((S,)), dma((S,)), dma((S,)), dma((S,)),
            dma((C, S)), dma((C, S)), dma((C, S)), dma((C, S)), dma((C, S)), dma((C, S)),
            dma((2, H)), dma((2, H)),
        ],
        compiler_params=pltpu.CompilerParams(collective_id=0, has_side_effects=True),
    )(w, xk, a, pos, b, key_up, value_up, out_proj)


def fits(shape, x, kv, w, a, key_up, value_up, out_proj):
    S, H = shape["seq"], shape["head"]
    hd, nope, kvr = key_up.shape
    rope = kv.shape[1] - kvr
    return (
        shape["groups"] == 2 and S > 1 and H == S and H % 2 == 0 and hd % (2 * S) == 0
        and (2 * (nope + rope)) % 128 == 0 and w.shape[0] % 32 == 0 and x.shape[0] % 16 == 0
        and nope % 128 == 0 and kvr % 128 == 0 and value_up.shape[2] % 128 == 0
        and x.shape[1] % 128 == 0 and out_proj.shape[1] % 256 == 0
    )


def on_device(
    query_latent_rows,
    key_value_latents,
    positions,
    query_up_weight,
    adapter_down_factor,
    adapter_up_factor,
    head_key_up_weight,
    head_value_up_weight,
    output_projection_weight,
):
    merged_query_weight = (
        query_up_weight.astype(jnp.float32)
        + jnp.dot(adapter_down_factor, adapter_up_factor, preferred_element_type=jnp.float32)
    ).astype(jnp.bfloat16)
    tok_rows = query_latent_rows.shape[0]
    queries = jnp.dot(
        query_latent_rows,
        lax.all_gather(merged_query_weight, "seq", axis=0, tiled=True),
        preferred_element_type=jnp.float32,
    )
    heads_dev = head_key_up_weight.shape[0]
    nope_dim = head_key_up_weight.shape[1]
    kv_rank = head_key_up_weight.shape[2]
    lat_width = key_value_latents.shape[1]
    score_scale = 1.0 / math.sqrt(nope_dim + lat_width - kv_rank)
    queries = queries.astype(jnp.bfloat16).reshape(tok_rows, heads_dev, -1)
    absorbed = jnp.einsum(
        "thn,hnk->thk",
        queries[:, :, :nope_dim],
        head_key_up_weight,
        preferred_element_type=jnp.float32,
    ).astype(jnp.bfloat16)
    full_query = jnp.concatenate([absorbed, queries[:, :, nope_dim:]], axis=2).reshape(
        tok_rows * heads_dev, lat_width
    )
    query_pos = jnp.repeat(positions, heads_dev)
    q_count = tok_rows * heads_dev
    row_max = jnp.full((q_count,), -1e30, jnp.float32)
    key_rows = lax.all_gather(key_value_latents, "seq", axis=0, tiled=True)
    key_pos = lax.all_gather(positions, "seq", axis=0, tiled=True)
    visible = key_pos[None, :] <= query_pos[:, None]
    scores = (
        lax.dot_general(
            full_query, key_rows, (((1,), (1,)), ((), ())), preferred_element_type=jnp.float32
        )
        * score_scale
    )
    scores = jnp.where(visible, scores, jnp.float32(-1e30))
    new_max = jnp.maximum(row_max, jnp.max(scores, axis=1))
    weights = jnp.where(visible, jnp.exp(scores - new_max[:, None]), jnp.float32(0.0))
    row_sum = jnp.sum(weights, axis=1)
    running = jnp.dot(
        weights.astype(jnp.bfloat16), key_rows[:, :kv_rank], preferred_element_type=jnp.float32
    )
    row_max, row_sum, running = (new_max, row_sum, running)
    context_output = (
        (running / row_sum[:, None]).astype(jnp.bfloat16).reshape(tok_rows, heads_dev, kv_rank)
    )
    heads_out = (
        jnp.einsum(
            "euw,uwz->euz", context_output, head_value_up_weight, preferred_element_type=jnp.float32
        )
        .astype(jnp.bfloat16)
        .reshape(tok_rows, -1)
    )
    partial_value = jnp.dot(
        lax.all_gather(heads_out, "seq", axis=0, tiled=True),
        output_projection_weight,
        preferred_element_type=jnp.float32,
    )
    mixed = lax.psum_scatter(
        partial_value.astype(jnp.bfloat16), "head", scatter_dimension=0, tiled=True
    )
    return (merged_query_weight, mixed)


def solution(mesh):
    placed = (
        P(("groups", "seq"), None),
        P(("groups", "seq"), None),
        P(("groups", "seq")),
        P("seq", "head"),
        P(("groups", "seq"), None),
        P("groups", "head"),
        P("head", None, None),
        P("head", None, None),
        P("head", "seq"),
    )

    def body(x, kv, positions, w, a, b, key_up, value_up, out_proj):
        if fits(mesh.shape, x, kv, w, a, key_up, value_up, out_proj):
            return fused(mesh.shape, x, kv, positions, w, a, b, key_up, value_up, out_proj)
        return on_device(x, kv, positions, w, a, b, key_up, value_up, out_proj)

    return jax.shard_map(
        body,
        mesh=mesh,
        in_specs=placed,
        out_specs=(P(("groups", "seq"), "head"), P(("groups", "head"), "seq")),
        check_vma=False,
    )
```

```python
import functools
import math

import jax
import jax.numpy as jnp
from jax import lax
from jax.experimental import pallas as pl
from jax.experimental.pallas import tpu as pltpu
from jax.sharding import PartitionSpec as P


MESH = pl.DeviceIdType.MESH


def fused_kernel(dims, pos, w, xk, a, b, key_up, value_up, out_proj, mixed,
                 b_v, pos_v, xk_all, a_all, pos_all, w_all, mm, ku_v, vu_v, op_v, heads, total,
                 part, pair, mid, got, loc, sx, rx, sy, ry, sa, ra, sb, rb, sp, rp, sw, rw, sv, rv, sh, rh,
                 st, rt, so, ro):
    S, H, C, T, KQ, NC, nope, rope, kvr, hp, cw, dcols, scale = dims
    qw = nope + rope
    half_k = KQ // 2
    half_x = xk.shape[1] // 2
    ql = S * KQ
    pw = (cw // qw) * (out_proj.shape[0] // (hp * S))
    heads_c = cw // qw
    vdim = out_proj.shape[0] // (hp * S)
    s = lax.axis_index("seq")
    g = lax.axis_index("groups")
    h = lax.axis_index("head")
    other = 1 - g
    pos_v[...] = jnp.full(pos_v.shape, pos[0], jnp.int32)
    core = lax.rem(h, 2)
    half_a = a.shape[0] // 2
    X = H // 2
    chip = h // 2
    sibling = h + 1 - 2 * core

    barrier = pltpu.get_barrier_semaphore()
    for k in range(1, S):
        pl.semaphore_signal(barrier, inc=1, device_id={"seq": lax.rem(s + k, S)}, device_id_type=MESH)
    for k in range(1, H):
        pl.semaphore_signal(barrier, inc=1, device_id={"head": lax.rem(h + k, H)}, device_id_type=MESH)
    pl.semaphore_signal(barrier, inc=1, device_id={"groups": other}, device_id_type=MESH)
    pl.semaphore_wait(barrier, S + H - 1)

    def remote(src, dst, ss, rs, **dev):
        return pltpu.make_async_remote_copy(
            src_ref=src, dst_ref=dst, send_sem=ss, recv_sem=rs, device_id=dev, device_id_type=MESH)

    sends = []

    def go(c):
        c.start()
        sends.append(c)
        return c

    def rows(i):
        return pl.ds(pl.multiple_of(i * T, T), T)

    def xcols(i):
        return pl.ds(pl.multiple_of(i * half_x, 128), half_x)

    def krows(i):
        return pl.ds(pl.multiple_of(i * half_k, 16), half_k)

    def arows(i):
        return pl.ds(pl.multiple_of(i * half_a, 16), half_a)

    class Line:
        def __init__(self, own, place, ss, rs, hook=None):
            self.own, self.place, self.ss, self.rs, self.hook = own, place, ss, rs, hook
            self.open = []

        def copy(self, src, q, slot, way):
            to = lax.rem(s + way + S, S)
            return remote(src, self.place(q), self.ss.at[slot], self.rs.at[q], seq=to)

        def send(self):
            for i, way in enumerate((1, -1)):
                has = s + 1 < S if way == 1 else s > 0
                self.start(has, self.own, s, i, way)

        def start(self, has, src, q, slot, way):
            @pl.when(has)
            def _():
                self.copy(src, q, slot, way).start()

            self.open.append((has, src, q, slot, way))

        def step(self, d):
            for i, way in enumerate((1, -1)):
                there = s >= d if way == 1 else s + d < S
                q = lax.rem(s - way * d + S, S)

                @pl.when(there)
                def _():
                    self.copy(self.place(q), q, i, way).wait_recv()
                    if self.hook is not None:
                        self.hook(q).start()

                on = s + 1 < S if way == 1 else s > 0
                if d < S - 1:
                    self.start(jnp.logical_and(there, on), self.place(q), q, 2 * d + i, way)

        def finish(self):
            for has, src, q, slot, way in self.open:
                @pl.when(has)
                def _():
                    self.copy(src, q, slot, way).wait_send()

    def x_place(q):
        return xk_all.at[rows(q), xcols(core)]

    def a_place(q):
        return a_all.at[q, arows(core)]

    def x_twin(q):
        return remote(x_place(q), x_place(q), sy.at[q], ry.at[q], head=sibling)

    def a_twin(q):
        return remote(a_place(q), a_place(q), sb.at[q], rb.at[q], head=sibling)

    def x_twin_in(q):
        there = xk_all.at[rows(q), xcols(1 - core)]
        return remote(there, there, sy.at[q], ry.at[q], head=sibling)

    def a_twin_in(q):
        there = a_all.at[q, arows(1 - core)]
        return remote(there, there, sb.at[q], rb.at[q], head=sibling)

    line_a = Line(a.at[arows(core)], a_place, sa, ra, a_twin)
    line_x = Line(xk.at[:, xcols(core)], x_place, sx, rx, x_twin)
    line_x.send()
    line_a.send()
    gp, gw = {}, {}
    for k in range(1, S):
        gp[k] = go(remote(pos_v, pos_all.at[s], sp.at[k], rp.at[k], seq=lax.rem(s + k, S)))

    def wcols(p, c):
        return pl.ds(pl.multiple_of(p * (cw * C) + c * cw, 128), cw)

    def scatter_w(c):
        for k in range(1, S):
            p = lax.rem(s + k, S)
            gw[c, k] = go(remote(
                w.at[krows(g), wcols(p, c)], w_all.at[c, s, krows(g)], sw.at[c, k], rw.at[c, k], seq=p))

    scatter_w(0)
    local = []

    def fetch(src, dst):
        cp = pltpu.make_async_copy(src, dst, loc.at[len(local)])
        cp.start()
        local.append(cp)
        return cp

    own = [fetch(b, b_v), fetch(xk, xk_all.at[rows(s)]), fetch(a, a_all.at[s]), fetch(pos_v, pos_all.at[s])]
    own += [fetch(w.at[:, wcols(s, c)], w_all.at[c, s]) for c in range(C)]
    own += [fetch(key_up.at[pl.ds(s * hp, hp)], ku_v), fetch(value_up.at[pl.ds(s * hp, hp)], vu_v)]
    ops = []
    for c in range(C):
        for i in range(S):
            ops.append(fetch(out_proj.at[pl.ds((i * hp + c * heads_c) * vdim, pw)], op_v.at[c, pl.ds(i * pw, pw)]))

    def forward(c):
        res = {}
        for k in range(1, S):
            q = lax.rem(s - k + S, S)
            gw[c, k].wait_recv()
            res[k] = go(remote(w_all.at[c, q, krows(g)], w_all.at[c, q, krows(g)], sv.at[c, k], rv.at[c, k], groups=other))
        return res

    mine = pl.ds(pl.multiple_of(s * pw, 128), pw)
    lines = []
    for c in range(C):
        def h_place(q, c=c):
            return heads.at[c, :, pl.ds(pl.multiple_of(q * pw, 128), pw)]

        lines.append(Line(h_place(s), h_place, sh.at[c], rh.at[c]))

    q_iota = lax.broadcasted_iota(jnp.int32, (S * T, 1), 0)
    k_iota = lax.broadcasted_iota(jnp.int32, (1, S * T), 1)

    def attend(c, between):
        for i in range(S):
            mm[i * KQ:(i + 1) * KQ] = (w_all[c, i].astype(jnp.float32) + lax.dot_general(
                a_all[i], b_v[:, wcols(s, c)], (((0,), (0,)), ((), ())), preferred_element_type=jnp.float32)).astype(jnp.bfloat16)
        queries = jnp.dot(xk_all[:, :ql], mm[...], preferred_element_type=jnp.float32)
        qpos = q_iota
        kpos = k_iota
        for i in range(S):
            start = pos_all[i, 0:1, 0:1] - i * T
            qpos = qpos + jnp.where(q_iota // T == i, start, 0)
            kpos = kpos + jnp.where(k_iota // T == i, start, 0)
        visible = kpos <= qpos
        lat = xk_all[:, ql:ql + kvr]
        key_rope = xk_all[:, ql + kvr:ql + kvr + rope]
        contract = (((1,), (1,)), ((), ()))
        for j in range(heads_c):
            qn = queries[:, j * qw:j * qw + nope].astype(jnp.bfloat16)
            qr = queries[:, j * qw + nope:(j + 1) * qw].astype(jnp.bfloat16)
            absorbed = jnp.dot(qn, ku_v[c * heads_c + j], preferred_element_type=jnp.float32).astype(jnp.bfloat16)
            scores = (lax.dot_general(absorbed, lat, contract, preferred_element_type=jnp.float32)
                      + lax.dot_general(qr, key_rope, contract, preferred_element_type=jnp.float32)) * scale
            scores = jnp.where(visible, scores, jnp.float32(-1e30))
            top = jnp.max(scores, axis=1, keepdims=True)
            weights = jnp.where(visible, jnp.exp(scores - top), jnp.float32(0.0))
            row_sum = jnp.sum(weights, axis=1, keepdims=True)
            context = jnp.dot(weights.astype(jnp.bfloat16), lat, preferred_element_type=jnp.float32)
            context = (context / row_sum).astype(jnp.bfloat16)
            res = jnp.dot(context, vu_v[c * heads_c + j], preferred_element_type=jnp.float32).astype(jnp.bfloat16)
            heads[c, :, pl.ds(pl.multiple_of(s * pw + j * vdim, 128), vdim)] = res
            if j == 0:
                between()

    for d in range(1, S):
        if d == S - 1:
            gv = forward(0)
        line_a.step(d)
        line_x.step(d)
        if d == 1:
            for c in range(1, C):
                scatter_w(c)
    for cp in own:
        cp.wait()
    for k in range(1, S):
        q = lax.rem(s + k, S)
        gp[k].wait_recv()
        a_twin_in(q).wait_recv()
        x_twin_in(q).wait_recv()
    for c in range(C):
        for k in range(1, S):
            gv[k].wait_recv()
        attend(c, (lambda: None) if c == 0 else (lambda: lines[c - 1].step(1)))
        if c < C - 1:
            gv = forward(c + 1)
        else:
            lines[c].send()
        if c > 0:
            for d in range(2, S):
                lines[c - 1].step(d)
        if c < C - 1:
            lines[c].send()
    for cp in ops:
        cp.wait()
    nb = 2
    bw = dcols // nb

    def trows(i):
        return pl.ds(pl.multiple_of(i * T, T), T)

    twin, cross = {}, {}

    def reduce_chip(i):
        for x in range(X):
            twin[i, x].wait_recv()
            mid[i, x] = (part[i, trows(2 * x + core)].astype(jnp.float32)
                         + pair[i, x].astype(jnp.float32)).astype(jnp.bfloat16)
        for k in range(1, X):
            x = lax.rem(chip + k, X)
            cross[i, k] = go(remote(mid.at[i, x], got.at[i, k], so.at[i, k], ro.at[i, k], head=2 * x + core))

    for c in range(C):
        for i in range(nb):
            cols = slice(i * bw, (i + 1) * bw)
            if c == C - 1 and i == 0:
                for d in range(2, S):
                    lines[c].step(d)
            acc = jnp.dot(heads[c], op_v[c, :, cols], preferred_element_type=jnp.float32)
            if c > 0:
                acc = acc + total[:, cols]
            if c < C - 1:
                total[:, cols] = acc
                if c == C - 2 and i == 0:
                    lines[C - 1].step(1)
            else:
                part[i] = acc.astype(jnp.bfloat16)
                for x in range(X):
                    twin[i, x] = go(remote(
                        part.at[i, trows(2 * x + 1 - core)], pair.at[i, x], st.at[i, x], rt.at[i, x], head=sibling))
                if i > 0:
                    reduce_chip(i - 1)
    reduce_chip(nb - 1)
    for i in range(nb):
        res = part[i, trows(h)].astype(jnp.float32) + pair[i, chip].astype(jnp.float32)
        for k in range(1, X):
            cross[i, k].wait_recv()
            res = res + got[i, k].astype(jnp.float32)
        mixed[:, i * bw:(i + 1) * bw] = res.astype(jnp.bfloat16)
    for cp in sends:
        cp.wait_send()
    for line in [line_x, line_a] + lines:
        line.finish()
    for k in range(1, S):
        q = lax.rem(s + k, S)
        a_twin(q).wait_send()
        x_twin(q).wait_send()


def merge_kernel(w, a, b, m):
    m[...] = (w[...].astype(jnp.float32) + lax.dot_general(
        a[...], b[...], (((0,), (0,)), ((), ())), preferred_element_type=jnp.float32)).astype(jnp.bfloat16)


def merge(w, a, b):
    KQ, NC = w.shape
    n = NC // 512 if NC % 512 == 0 else 1
    return pl.pallas_call(
        merge_kernel,
        grid=(n,),
        out_shape=jax.ShapeDtypeStruct(w.shape, w.dtype),
        in_specs=[pl.BlockSpec((KQ, NC // n), lambda i: (0, i)), pl.BlockSpec(a.shape, lambda i: (0, 0)),
                  pl.BlockSpec((b.shape[0], NC // n), lambda i: (0, i))],
        out_specs=pl.BlockSpec((KQ, NC // n), lambda i: (0, i)),
    )(w, a, b)


def fused(mesh_shape, x, kv, positions, w, a, b, key_up, value_up, out_proj):
    S, H = mesh_shape["seq"], mesh_shape["head"]
    T, ql = x.shape
    KQ, NC = w.shape
    hd, nope, kvr = key_up.shape
    rope = kv.shape[1] - kvr
    vdim = value_up.shape[2]
    hp = hd // S
    heads_c = 2
    C = hp // heads_c
    cw = heads_c * (nope + rope)
    dcols = out_proj.shape[1]
    width = ql + kv.shape[1]
    full = -(-width // 256) * 256
    xk = jnp.concatenate([x, kv, jnp.zeros((T, full - width), x.dtype)], axis=1)
    at = jnp.transpose(a)
    scale = 1.0 / math.sqrt(nope + rope)
    dims = (S, H, C, T, KQ, NC, nope, rope, kvr, hp, cw, dcols, scale)
    bf, f32 = jnp.bfloat16, jnp.float32
    dma = pltpu.SemaphoreType.DMA
    nloc = 4 + C + 2 + C * S
    pw = heads_c * vdim
    mixed = pl.pallas_call(
        functools.partial(fused_kernel, dims),
        out_shape=jax.ShapeDtypeStruct((T, dcols), bf),
        in_specs=[pl.BlockSpec(memory_space=pltpu.SMEM)] + [pl.BlockSpec(memory_space=pl.ANY)] * 7,
        out_specs=pl.BlockSpec(memory_space=pltpu.VMEM),
        scratch_shapes=[
            pltpu.VMEM(b.shape, bf), pltpu.VMEM((8, 128), jnp.int32),
            pltpu.VMEM((S * T, full), bf), pltpu.VMEM((S,) + at.shape, bf), pltpu.VMEM((S, 8, 128), jnp.int32),
            pltpu.VMEM((C, S, KQ, cw), bf), pltpu.VMEM((S * KQ, cw), bf),
            pltpu.VMEM((hp, nope, kvr), bf), pltpu.VMEM((hp, kvr, vdim), bf),
            pltpu.VMEM((C, S * pw, dcols), bf), pltpu.VMEM((C, S * T, S * pw), bf), pltpu.VMEM((S * T, dcols), f32),
            pltpu.VMEM((2, S * T, dcols // 2), bf), pltpu.VMEM((2, H // 2, T, dcols // 2), bf),
            pltpu.VMEM((2, H // 2, T, dcols // 2), bf), pltpu.VMEM((2, H // 2, T, dcols // 2), bf),
            dma((nloc,)),
            dma((2 * S,)), dma((S,)), dma((S,)), dma((S,)), dma((2 * S,)), dma((S,)), dma((S,)), dma((S,)),
            dma((S,)), dma((S,)),
            dma((C, S)), dma((C, S)), dma((C, S)), dma((C, S)), dma((C, 2 * S)), dma((C, S)),
            dma((2, H // 2)), dma((2, H // 2)), dma((2, H // 2)), dma((2, H // 2)),
        ],
        compiler_params=pltpu.CompilerParams(collective_id=0, has_side_effects=True),
    )(positions, w, xk, at, b, key_up, value_up, out_proj)
    return merge(w, at, b), mixed


def fits(shape, x, kv, w, a, key_up, value_up, out_proj):
    S, H = shape["seq"], shape["head"]
    hd, nope, kvr = key_up.shape
    rope = kv.shape[1] - kvr
    return (
        shape["groups"] == 2 and S > 1 and H == S and H % 2 == 0 and hd % (4 * S) == 0
        and (2 * (nope + rope)) % 128 == 0 and w.shape[0] % 32 == 0 and a.shape[1] % 32 == 0 and x.shape[0] % 16 == 0
        and nope % 128 == 0 and kvr % 128 == 0 and value_up.shape[2] % 128 == 0
        and x.shape[1] % 128 == 0 and out_proj.shape[1] % 256 == 0
    )


def on_device(
    query_latent_rows,
    key_value_latents,
    positions,
    query_up_weight,
    adapter_down_factor,
    adapter_up_factor,
    head_key_up_weight,
    head_value_up_weight,
    output_projection_weight,
):
    merged_query_weight = (
        query_up_weight.astype(jnp.float32)
        + jnp.dot(adapter_down_factor, adapter_up_factor, preferred_element_type=jnp.float32)
    ).astype(jnp.bfloat16)
    tok_rows = query_latent_rows.shape[0]
    queries = jnp.dot(
        query_latent_rows,
        lax.all_gather(merged_query_weight, "seq", axis=0, tiled=True),
        preferred_element_type=jnp.float32,
    )
    heads_dev = head_key_up_weight.shape[0]
    nope_dim = head_key_up_weight.shape[1]
    kv_rank = head_key_up_weight.shape[2]
    lat_width = key_value_latents.shape[1]
    score_scale = 1.0 / math.sqrt(nope_dim + lat_width - kv_rank)
    queries = queries.astype(jnp.bfloat16).reshape(tok_rows, heads_dev, -1)
    absorbed = jnp.einsum(
        "thn,hnk->thk",
        queries[:, :, :nope_dim],
        head_key_up_weight,
        preferred_element_type=jnp.float32,
    ).astype(jnp.bfloat16)
    full_query = jnp.concatenate([absorbed, queries[:, :, nope_dim:]], axis=2).reshape(
        tok_rows * heads_dev, lat_width
    )
    query_pos = jnp.repeat(positions, heads_dev)
    q_count = tok_rows * heads_dev
    row_max = jnp.full((q_count,), -1e30, jnp.float32)
    key_rows = lax.all_gather(key_value_latents, "seq", axis=0, tiled=True)
    key_pos = lax.all_gather(positions, "seq", axis=0, tiled=True)
    visible = key_pos[None, :] <= query_pos[:, None]
    scores = (
        lax.dot_general(
            full_query, key_rows, (((1,), (1,)), ((), ())), preferred_element_type=jnp.float32
        )
        * score_scale
    )
    scores = jnp.where(visible, scores, jnp.float32(-1e30))
    new_max = jnp.maximum(row_max, jnp.max(scores, axis=1))
    weights = jnp.where(visible, jnp.exp(scores - new_max[:, None]), jnp.float32(0.0))
    row_sum = jnp.sum(weights, axis=1)
    running = jnp.dot(
        weights.astype(jnp.bfloat16), key_rows[:, :kv_rank], preferred_element_type=jnp.float32
    )
    row_max, row_sum, running = (new_max, row_sum, running)
    context_output = (
        (running / row_sum[:, None]).astype(jnp.bfloat16).reshape(tok_rows, heads_dev, kv_rank)
    )
    heads_out = (
        jnp.einsum(
            "euw,uwz->euz", context_output, head_value_up_weight, preferred_element_type=jnp.float32
        )
        .astype(jnp.bfloat16)
        .reshape(tok_rows, -1)
    )
    partial_value = jnp.dot(
        lax.all_gather(heads_out, "seq", axis=0, tiled=True),
        output_projection_weight,
        preferred_element_type=jnp.float32,
    )
    mixed = lax.psum_scatter(
        partial_value.astype(jnp.bfloat16), "head", scatter_dimension=0, tiled=True
    )
    return (merged_query_weight, mixed)


def solution(mesh):
    placed = (
        P(("groups", "seq"), None),
        P(("groups", "seq"), None),
        P(("groups", "seq")),
        P("seq", "head"),
        P(("groups", "seq"), None),
        P("groups", "head"),
        P("head", None, None),
        P("head", None, None),
        P("head", "seq"),
    )

    def body(x, kv, positions, w, a, b, key_up, value_up, out_proj):
        if fits(mesh.shape, x, kv, w, a, key_up, value_up, out_proj):
            return fused(mesh.shape, x, kv, positions, w, a, b, key_up, value_up, out_proj)
        return on_device(x, kv, positions, w, a, b, key_up, value_up, out_proj)

    return jax.shard_map(
        body,
        mesh=mesh,
        in_specs=placed,
        out_specs=(P(("groups", "seq"), "head"), P(("groups", "head"), "seq")),
        check_vma=False,
    )
```

```python
import functools
import math

import jax
import jax.numpy as jnp
from jax import lax
from jax.experimental import pallas as pl
from jax.experimental.pallas import tpu as pltpu
from jax.sharding import PartitionSpec as P


MESH = pl.DeviceIdType.MESH


def fused_kernel(dims, pos, w, xk, a, b, key_up, value_up, out_proj, merged, mixed,
                 w_v, m_v, b_v, pos_v, xk_all, a_all, pos_all, w_all, mm, ku_v, vu_v, op_v, heads, total,
                 part, pair, mid, got, loc, sx, rx, sy, ry, sa, ra, sb, rb, sp, rp, sw, rw, sv, rv, sh, rh,
                 st, rt, so, ro):
    S, H, C, T, KQ, NC, nope, rope, kvr, hp, cw, dcols, scale = dims
    qw = nope + rope
    half_k = KQ // 2
    part_x = xk.shape[1] // H
    ql = S * KQ
    pw = (cw // qw) * (out_proj.shape[0] // (hp * S))
    heads_c = cw // qw
    vdim = out_proj.shape[0] // (hp * S)
    s = lax.axis_index("seq")
    g = lax.axis_index("groups")
    h = lax.axis_index("head")
    other = 1 - g
    pos_v[...] = jnp.full(pos_v.shape, pos[0], jnp.int32)
    core = lax.rem(h, 2)
    part_a = a.shape[0] // H
    X = H // 2
    chip = h // 2
    sibling = h + 1 - 2 * core

    barrier = pltpu.get_barrier_semaphore()
    for k in range(1, S):
        pl.semaphore_signal(barrier, inc=1, device_id={"seq": lax.rem(s + k, S)}, device_id_type=MESH)
    for k in range(1, H):
        pl.semaphore_signal(barrier, inc=1, device_id={"head": lax.rem(h + k, H)}, device_id_type=MESH)
    pl.semaphore_signal(barrier, inc=1, device_id={"groups": other}, device_id_type=MESH)
    pl.semaphore_wait(barrier, S + H - 1)

    def remote(src, dst, ss, rs, **dev):
        return pltpu.make_async_remote_copy(
            src_ref=src, dst_ref=dst, send_sem=ss, recv_sem=rs, device_id=dev, device_id_type=MESH)

    sends = []

    def go(c):
        c.start()
        sends.append(c)
        return c

    def rows(i):
        return pl.ds(pl.multiple_of(i * T, T), T)

    def xcols(i):
        return pl.ds(pl.multiple_of(i * part_x, 128), part_x)

    def krows(i):
        return pl.ds(pl.multiple_of(i * half_k, 16), half_k)

    def arows(i):
        return pl.ds(pl.multiple_of(i * part_a, 16), part_a)

    class Line:
        def __init__(self, own, place, ss, rs, hook=None):
            self.own, self.place, self.ss, self.rs, self.hook = own, place, ss, rs, hook
            self.open = []

        def copy(self, src, q, slot, way):
            to = lax.rem(s + way + S, S)
            return remote(src, self.place(q), self.ss.at[slot], self.rs.at[q], seq=to)

        def send(self):
            for i, way in enumerate((1, -1)):
                has = s + 1 < S if way == 1 else s > 0
                self.start(has, self.own, s, i, way)

        def start(self, has, src, q, slot, way):
            @pl.when(has)
            def _():
                self.copy(src, q, slot, way).start()

            self.open.append((has, src, q, slot, way))

        def step(self, d):
            for i, way in enumerate((1, -1)):
                there = s >= d if way == 1 else s + d < S
                q = lax.rem(s - way * d + S, S)

                @pl.when(there)
                def _():
                    self.copy(self.place(q), q, i, way).wait_recv()
                    if self.hook is not None:
                        self.hook(q).start()

                on = s + 1 < S if way == 1 else s > 0
                if d < S - 1:
                    self.start(jnp.logical_and(there, on), self.place(q), q, 2 * d + i, way)

        def finish(self):
            for has, src, q, slot, way in self.open:
                @pl.when(has)
                def _():
                    self.copy(src, q, slot, way).wait_send()

    gp, gw, gx, ga, yx, ya = {}, {}, {}, {}, {}, {}
    for k in range(1, S):
        p = lax.rem(s + k, S)
        gx[k] = go(remote(xk.at[:, xcols(h)], xk_all.at[rows(s), xcols(h)], sx.at[k], rx.at[k], seq=p))
        ga[k] = go(remote(a.at[arows(h)], a_all.at[s, arows(h)], sa.at[k], ra.at[k], seq=p))
        gp[k] = go(remote(pos_v, pos_all.at[s], sp.at[k], rp.at[k], seq=p))

    def wcols(p, c):
        return pl.ds(pl.multiple_of(p * (cw * C) + c * cw, 128), cw)

    def scatter_w(c):
        for k in range(1, S):
            p = lax.rem(s + k, S)
            gw[c, k] = go(remote(
                w.at[krows(g), wcols(p, c)], w_all.at[c, s, krows(g)], sw.at[c, k], rw.at[c, k], seq=p))

    for c in range(C):
        scatter_w(c)
    local = []

    def fetch(src, dst):
        cp = pltpu.make_async_copy(src, dst, loc.at[len(local)])
        cp.start()
        local.append(cp)
        return cp

    own = [fetch(b, b_v), fetch(w, w_v), fetch(a, a_all.at[s]), fetch(xk, xk_all.at[rows(s)]), fetch(pos_v, pos_all.at[s])]
    own += [fetch(w.at[:, wcols(s, c)], w_all.at[c, s]) for c in range(C)]
    own += [fetch(key_up.at[pl.ds(s * hp, hp)], ku_v), fetch(value_up.at[pl.ds(s * hp, hp)], vu_v)]
    ops = []
    for c in range(C):
        for i in range(S):
            ops.append(fetch(out_proj.at[pl.ds((i * hp + c * heads_c) * vdim, pw)], op_v.at[c, pl.ds(i * pw, pw)]))

    def forward(c):
        res = {}
        for k in range(1, S):
            q = lax.rem(s - k + S, S)
            gw[c, k].wait_recv()
            res[k] = go(remote(w_all.at[c, q, krows(g)], w_all.at[c, q, krows(g)], sv.at[c, k], rv.at[c, k], groups=other))
        return res

    mine = pl.ds(pl.multiple_of(s * pw, 128), pw)
    lines = []
    for c in range(C):
        def h_place(q, c=c):
            return heads.at[c, :, pl.ds(pl.multiple_of(q * pw, 128), pw)]

        lines.append(Line(h_place(s), h_place, sh.at[c], rh.at[c]))

    q_iota = lax.broadcasted_iota(jnp.int32, (S * T, 1), 0)
    k_iota = lax.broadcasted_iota(jnp.int32, (1, S * T), 1)

    def attend(c, between):
        for i in range(S):
            mm[i * KQ:(i + 1) * KQ] = (w_all[c, i].astype(jnp.float32) + lax.dot_general(
                a_all[i], b_v[:, wcols(s, c)], (((0,), (0,)), ((), ())), preferred_element_type=jnp.float32)).astype(jnp.bfloat16)
        queries = jnp.dot(xk_all[:, :ql], mm[...], preferred_element_type=jnp.float32)
        qpos = q_iota
        kpos = k_iota
        for i in range(S):
            start = pos_all[i, 0:1, 0:1] - i * T
            qpos = qpos + jnp.where(q_iota // T == i, start, 0)
            kpos = kpos + jnp.where(k_iota // T == i, start, 0)
        visible = kpos <= qpos
        lat = xk_all[:, ql:ql + kvr]
        key_rope = xk_all[:, ql + kvr:ql + kvr + rope]
        contract = (((1,), (1,)), ((), ()))
        for j in range(heads_c):
            qn = queries[:, j * qw:j * qw + nope].astype(jnp.bfloat16)
            qr = queries[:, j * qw + nope:(j + 1) * qw].astype(jnp.bfloat16)
            absorbed = jnp.dot(qn, ku_v[c * heads_c + j], preferred_element_type=jnp.float32).astype(jnp.bfloat16)
            scores = (lax.dot_general(absorbed, lat, contract, preferred_element_type=jnp.float32)
                      + lax.dot_general(qr, key_rope, contract, preferred_element_type=jnp.float32)) * scale
            scores = jnp.where(visible, scores, jnp.float32(-1e30))
            top = jnp.max(scores, axis=1, keepdims=True)
            weights = jnp.where(visible, jnp.exp(scores - top), jnp.float32(0.0))
            row_sum = jnp.sum(weights, axis=1, keepdims=True)
            context = jnp.dot(weights.astype(jnp.bfloat16), lat, preferred_element_type=jnp.float32)
            context = (context / row_sum).astype(jnp.bfloat16)
            res = jnp.dot(context, vu_v[c * heads_c + j], preferred_element_type=jnp.float32).astype(jnp.bfloat16)
            heads[c, :, pl.ds(pl.multiple_of(s * pw + j * vdim, 128), vdim)] = res
            if j == 0:
                between()

    for k in range(1, S):
        q = lax.rem(s - k + S, S)
        gx[k].wait_recv()
        for j in range(1, H):
            to = lax.rem(h + j, H)
            yx[k, j] = go(remote(
                xk_all.at[rows(q), xcols(h)], xk_all.at[rows(q), xcols(h)], sy.at[k, j], ry.at[k, j], head=to))
        ga[k].wait_recv()
        for j in range(1, H):
            to = lax.rem(h + j, H)
            ya[k, j] = go(remote(
                a_all.at[q, arows(h)], a_all.at[q, arows(h)], sb.at[k, j], rb.at[k, j], head=to))
    for cp in own:
        cp.wait()

    def merge_cols(i, carry):
        cols = pl.ds(pl.multiple_of(i * cw, 128), cw)
        m_v[:, cols] = (w_v[:, cols].astype(jnp.float32) + lax.dot_general(
            a_all[s], b_v[:, cols], (((0,), (0,)), ((), ())), preferred_element_type=jnp.float32)).astype(jnp.bfloat16)
        return carry

    lax.fori_loop(0, NC // cw, merge_cols, 0)
    out_m = pltpu.make_async_copy(m_v, merged, loc.at[len(local)])
    out_m.start()
    gv = forward(0)
    for k in range(1, S):
        gp[k].wait_recv()
        for j in range(1, H):
            ya[k, j].wait_recv()
            yx[k, j].wait_recv()
    for c in range(C):
        for k in range(1, S):
            gv[k].wait_recv()
        attend(c, (lambda: None) if c == 0 else (lambda: lines[c - 1].step(1)))
        if c < C - 1:
            gv = forward(c + 1)
        else:
            lines[c].send()
        if c > 0:
            for d in range(2, S):
                lines[c - 1].step(d)
        if c < C - 1:
            lines[c].send()
    for cp in ops:
        cp.wait()
    nb = 2
    bw = dcols // nb

    def trows(i):
        return pl.ds(pl.multiple_of(i * T, T), T)

    twin, cross = {}, {}

    def reduce_chip(i):
        for x in range(X):
            twin[i, x].wait_recv()
            mid[i, x] = (part[i, trows(2 * x + core)].astype(jnp.float32)
                         + pair[i, x].astype(jnp.float32)).astype(jnp.bfloat16)
        for k in range(1, X):
            x = lax.rem(chip + k, X)
            cross[i, k] = go(remote(mid.at[i, x], got.at[i, k], so.at[i, k], ro.at[i, k], head=2 * x + core))

    for c in range(C):
        for i in range(nb):
            cols = slice(i * bw, (i + 1) * bw)
            if c == C - 1 and i == 0:
                for d in range(2, S):
                    lines[c].step(d)
            acc = jnp.dot(heads[c], op_v[c, :, cols], preferred_element_type=jnp.float32)
            if c > 0:
                acc = acc + total[:, cols]
            if c < C - 1:
                total[:, cols] = acc
                if c == C - 2 and i == 0:
                    lines[C - 1].step(1)
            else:
                part[i] = acc.astype(jnp.bfloat16)
                for x in range(X):
                    twin[i, x] = go(remote(
                        part.at[i, trows(2 * x + 1 - core)], pair.at[i, x], st.at[i, x], rt.at[i, x], head=sibling))
                if i > 0:
                    reduce_chip(i - 1)
    reduce_chip(nb - 1)
    for i in range(nb):
        res = part[i, trows(h)].astype(jnp.float32) + pair[i, chip].astype(jnp.float32)
        for k in range(1, X):
            cross[i, k].wait_recv()
            res = res + got[i, k].astype(jnp.float32)
        mixed[:, i * bw:(i + 1) * bw] = res.astype(jnp.bfloat16)
    for cp in sends:
        cp.wait_send()
    for line in lines:
        line.finish()
    out_m.wait()


def fused(mesh_shape, x, kv, positions, w, a, b, key_up, value_up, out_proj):
    S, H = mesh_shape["seq"], mesh_shape["head"]
    T, ql = x.shape
    KQ, NC = w.shape
    hd, nope, kvr = key_up.shape
    rope = kv.shape[1] - kvr
    vdim = value_up.shape[2]
    hp = hd // S
    heads_c = 2
    C = hp // heads_c
    cw = heads_c * (nope + rope)
    dcols = out_proj.shape[1]
    width = ql + kv.shape[1]
    full = -(-width // (128 * H)) * (128 * H)
    xk = jnp.concatenate([x, kv, jnp.zeros((T, full - width), x.dtype)], axis=1)
    at = jnp.transpose(a)
    scale = 1.0 / math.sqrt(nope + rope)
    dims = (S, H, C, T, KQ, NC, nope, rope, kvr, hp, cw, dcols, scale)
    bf, f32 = jnp.bfloat16, jnp.float32
    dma = pltpu.SemaphoreType.DMA
    nloc = 5 + C + 2 + C * S + 1
    pw = heads_c * vdim
    return pl.pallas_call(
        functools.partial(fused_kernel, dims),
        out_shape=(jax.ShapeDtypeStruct((KQ, NC), bf), jax.ShapeDtypeStruct((T, dcols), bf)),
        in_specs=[pl.BlockSpec(memory_space=pltpu.SMEM)] + [pl.BlockSpec(memory_space=pl.ANY)] * 7,
        out_specs=(pl.BlockSpec(memory_space=pl.ANY), pl.BlockSpec(memory_space=pltpu.VMEM)),
        scratch_shapes=[
            pltpu.VMEM((KQ, NC), bf), pltpu.VMEM((KQ, NC), bf),
            pltpu.VMEM(b.shape, bf), pltpu.VMEM((8, 128), jnp.int32),
            pltpu.VMEM((S * T, full), bf), pltpu.VMEM((S,) + at.shape, bf), pltpu.VMEM((S, 8, 128), jnp.int32),
            pltpu.VMEM((C, S, KQ, cw), bf), pltpu.VMEM((S * KQ, cw), bf),
            pltpu.VMEM((hp, nope, kvr), bf), pltpu.VMEM((hp, kvr, vdim), bf),
            pltpu.VMEM((C, S * pw, dcols), bf), pltpu.VMEM((C, S * T, S * pw), bf), pltpu.VMEM((S * T, dcols), f32),
            pltpu.VMEM((2, S * T, dcols // 2), bf), pltpu.VMEM((2, H // 2, T, dcols // 2), bf),
            pltpu.VMEM((2, H // 2, T, dcols // 2), bf), pltpu.VMEM((2, H // 2, T, dcols // 2), bf),
            dma((nloc,)),
            dma((S,)), dma((S,)), dma((S, H)), dma((S, H)), dma((S,)), dma((S,)), dma((S, H)), dma((S, H)),
            dma((S,)), dma((S,)),
            dma((C, S)), dma((C, S)), dma((C, S)), dma((C, S)), dma((C, 2 * S)), dma((C, S)),
            dma((2, H // 2)), dma((2, H // 2)), dma((2, H // 2)), dma((2, H // 2)),
        ],
        compiler_params=pltpu.CompilerParams(collective_id=0, has_side_effects=True),
    )(positions, w, xk, at, b, key_up, value_up, out_proj)


def fits(shape, x, kv, w, a, key_up, value_up, out_proj):
    S, H = shape["seq"], shape["head"]
    hd, nope, kvr = key_up.shape
    rope = kv.shape[1] - kvr
    return (
        shape["groups"] == 2 and S > 1 and H == S and H % 2 == 0 and hd % (4 * S) == 0
        and (2 * (nope + rope)) % 128 == 0 and w.shape[0] % 32 == 0 and a.shape[1] % (16 * H) == 0 and x.shape[0] % 16 == 0
        and nope % 128 == 0 and kvr % 128 == 0 and value_up.shape[2] % 128 == 0
        and x.shape[1] % 128 == 0 and out_proj.shape[1] % 256 == 0
    )


def on_device(
    query_latent_rows,
    key_value_latents,
    positions,
    query_up_weight,
    adapter_down_factor,
    adapter_up_factor,
    head_key_up_weight,
    head_value_up_weight,
    output_projection_weight,
):
    merged_query_weight = (
        query_up_weight.astype(jnp.float32)
        + jnp.dot(adapter_down_factor, adapter_up_factor, preferred_element_type=jnp.float32)
    ).astype(jnp.bfloat16)
    tok_rows = query_latent_rows.shape[0]
    queries = jnp.dot(
        query_latent_rows,
        lax.all_gather(merged_query_weight, "seq", axis=0, tiled=True),
        preferred_element_type=jnp.float32,
    )
    heads_dev = head_key_up_weight.shape[0]
    nope_dim = head_key_up_weight.shape[1]
    kv_rank = head_key_up_weight.shape[2]
    lat_width = key_value_latents.shape[1]
    score_scale = 1.0 / math.sqrt(nope_dim + lat_width - kv_rank)
    queries = queries.astype(jnp.bfloat16).reshape(tok_rows, heads_dev, -1)
    absorbed = jnp.einsum(
        "thn,hnk->thk",
        queries[:, :, :nope_dim],
        head_key_up_weight,
        preferred_element_type=jnp.float32,
    ).astype(jnp.bfloat16)
    full_query = jnp.concatenate([absorbed, queries[:, :, nope_dim:]], axis=2).reshape(
        tok_rows * heads_dev, lat_width
    )
    query_pos = jnp.repeat(positions, heads_dev)
    q_count = tok_rows * heads_dev
    row_max = jnp.full((q_count,), -1e30, jnp.float32)
    key_rows = lax.all_gather(key_value_latents, "seq", axis=0, tiled=True)
    key_pos = lax.all_gather(positions, "seq", axis=0, tiled=True)
    visible = key_pos[None, :] <= query_pos[:, None]
    scores = (
        lax.dot_general(
            full_query, key_rows, (((1,), (1,)), ((), ())), preferred_element_type=jnp.float32
        )
        * score_scale
    )
    scores = jnp.where(visible, scores, jnp.float32(-1e30))
    new_max = jnp.maximum(row_max, jnp.max(scores, axis=1))
    weights = jnp.where(visible, jnp.exp(scores - new_max[:, None]), jnp.float32(0.0))
    row_sum = jnp.sum(weights, axis=1)
    running = jnp.dot(
        weights.astype(jnp.bfloat16), key_rows[:, :kv_rank], preferred_element_type=jnp.float32
    )
    row_max, row_sum, running = (new_max, row_sum, running)
    context_output = (
        (running / row_sum[:, None]).astype(jnp.bfloat16).reshape(tok_rows, heads_dev, kv_rank)
    )
    heads_out = (
        jnp.einsum(
            "euw,uwz->euz", context_output, head_value_up_weight, preferred_element_type=jnp.float32
        )
        .astype(jnp.bfloat16)
        .reshape(tok_rows, -1)
    )
    partial_value = jnp.dot(
        lax.all_gather(heads_out, "seq", axis=0, tiled=True),
        output_projection_weight,
        preferred_element_type=jnp.float32,
    )
    mixed = lax.psum_scatter(
        partial_value.astype(jnp.bfloat16), "head", scatter_dimension=0, tiled=True
    )
    return (merged_query_weight, mixed)


def solution(mesh):
    placed = (
        P(("groups", "seq"), None),
        P(("groups", "seq"), None),
        P(("groups", "seq")),
        P("seq", "head"),
        P(("groups", "seq"), None),
        P("groups", "head"),
        P("head", None, None),
        P("head", None, None),
        P("head", "seq"),
    )

    def body(x, kv, positions, w, a, b, key_up, value_up, out_proj):
        if fits(mesh.shape, x, kv, w, a, key_up, value_up, out_proj):
            return fused(mesh.shape, x, kv, positions, w, a, b, key_up, value_up, out_proj)
        return on_device(x, kv, positions, w, a, b, key_up, value_up, out_proj)

    return jax.shard_map(
        body,
        mesh=mesh,
        in_specs=placed,
        out_specs=(P(("groups", "seq"), "head"), P(("groups", "head"), "seq")),
        check_vma=False,
    )
```

```python
import functools
import math

import jax
import jax.numpy as jnp
from jax import lax
from jax.experimental import pallas as pl
from jax.experimental.pallas import tpu as pltpu
from jax.sharding import PartitionSpec as P


MESH = pl.DeviceIdType.MESH


def fused_kernel(dims, pos, w, xk, a, b, key_up, value_up, out_proj, merged, mixed,
                 w_v, m_v, b_v, pos_v, xk_all, a_all, pos_all, w_all, mm, ku_v, vu_v, op_v, heads, total,
                 part, pair, mid, got, loc, sx, rx, sy, ry, sa, ra, sb, rb, sp, rp, sw, rw, sv, rv, sh, rh,
                 st, rt, so, ro):
    S, H, C, T, KQ, NC, nope, rope, kvr, hp, cw, dcols, scale = dims
    qw = nope + rope
    half_k = KQ // 2
    part_x = xk.shape[1] // H
    ql = S * KQ
    pw = (cw // qw) * (out_proj.shape[0] // (hp * S))
    heads_c = cw // qw
    vdim = out_proj.shape[0] // (hp * S)
    s = lax.axis_index("seq")
    g = lax.axis_index("groups")
    h = lax.axis_index("head")
    other = 1 - g
    pos_v[...] = jnp.full(pos_v.shape, pos[0], jnp.int32)
    core = lax.rem(h, 2)
    part_a = a.shape[0] // H
    X = H // 2
    chip = h // 2
    sibling = h + 1 - 2 * core

    barrier = pltpu.get_barrier_semaphore()
    for k in range(1, S):
        pl.semaphore_signal(barrier, inc=1, device_id={"seq": lax.rem(s + k, S)}, device_id_type=MESH)
    for k in range(1, H):
        pl.semaphore_signal(barrier, inc=1, device_id={"head": lax.rem(h + k, H)}, device_id_type=MESH)
    pl.semaphore_signal(barrier, inc=1, device_id={"groups": other}, device_id_type=MESH)
    pl.semaphore_wait(barrier, S + H - 1)

    def remote(src, dst, ss, rs, **dev):
        return pltpu.make_async_remote_copy(
            src_ref=src, dst_ref=dst, send_sem=ss, recv_sem=rs, device_id=dev, device_id_type=MESH)

    sends = []

    def go(c):
        c.start()
        sends.append(c)
        return c

    def rows(i):
        return pl.ds(pl.multiple_of(i * T, T), T)

    def xcols(i):
        return pl.ds(pl.multiple_of(i * part_x, 128), part_x)

    def krows(i):
        return pl.ds(pl.multiple_of(i * half_k, 16), half_k)

    def arows(i):
        return pl.ds(pl.multiple_of(i * part_a, 16), part_a)

    class Line:
        def __init__(self, own, place, ss, rs, hook=None):
            self.own, self.place, self.ss, self.rs, self.hook = own, place, ss, rs, hook
            self.open = []

        def copy(self, src, q, slot, way):
            to = lax.rem(s + way + S, S)
            return remote(src, self.place(q), self.ss.at[slot], self.rs.at[q], seq=to)

        def send(self):
            for i, way in enumerate((1, -1)):
                has = s + 1 < S if way == 1 else s > 0
                self.start(has, self.own, s, i, way)

        def start(self, has, src, q, slot, way):
            @pl.when(has)
            def _():
                self.copy(src, q, slot, way).start()

            self.open.append((has, src, q, slot, way))

        def step(self, d):
            for i, way in enumerate((1, -1)):
                there = s >= d if way == 1 else s + d < S
                q = lax.rem(s - way * d + S, S)

                @pl.when(there)
                def _():
                    self.copy(self.place(q), q, i, way).wait_recv()
                    if self.hook is not None:
                        self.hook(q).start()

                on = s + 1 < S if way == 1 else s > 0
                if d < S - 1:
                    self.start(jnp.logical_and(there, on), self.place(q), q, 2 * d + i, way)

        def finish(self):
            for has, src, q, slot, way in self.open:
                @pl.when(has)
                def _():
                    self.copy(src, q, slot, way).wait_send()

    gp, gw, gx, ga, yx, ya = {}, {}, {}, {}, {}, {}
    for k in range(1, S):
        p = lax.rem(s + k, S)
        gx[k] = go(remote(xk.at[:, xcols(h)], xk_all.at[rows(s), xcols(h)], sx.at[k], rx.at[k], seq=p))
        ga[k] = go(remote(a.at[arows(h)], a_all.at[s, arows(h)], sa.at[k], ra.at[k], seq=p))
        gp[k] = go(remote(pos_v, pos_all.at[s], sp.at[k], rp.at[k], seq=p))

    def wcols(p, c):
        return pl.ds(pl.multiple_of(p * (cw * C) + c * cw, 128), cw)

    def scatter_w(c):
        for k in range(1, S):
            p = lax.rem(s + k, S)
            gw[c, k] = go(remote(
                w.at[krows(g), wcols(p, c)], w_all.at[c, s, krows(g)], sw.at[c, k], rw.at[c, k], seq=p))

    for c in range(C):
        scatter_w(c)
    local = []

    def fetch(src, dst):
        cp = pltpu.make_async_copy(src, dst, loc.at[len(local)])
        cp.start()
        local.append(cp)
        return cp

    own = [fetch(b, b_v), fetch(w, w_v), fetch(a, a_all.at[s]), fetch(xk, xk_all.at[rows(s)]), fetch(pos_v, pos_all.at[s])]
    own += [fetch(w.at[:, wcols(s, c)], w_all.at[c, s]) for c in range(C)]
    own += [fetch(key_up.at[pl.ds(s * hp, hp)], ku_v), fetch(value_up.at[pl.ds(s * hp, hp)], vu_v)]
    ops = []
    for c in range(C):
        for i in range(S):
            ops.append(fetch(out_proj.at[pl.ds((i * hp + c * heads_c) * vdim, pw)], op_v.at[c, pl.ds(i * pw, pw)]))

    def forward(c):
        res = {}
        for k in range(1, S):
            q = lax.rem(s - k + S, S)
            gw[c, k].wait_recv()
            res[k] = go(remote(w_all.at[c, q, krows(g)], w_all.at[c, q, krows(g)], sv.at[c, k], rv.at[c, k], groups=other))
        return res

    mine = pl.ds(pl.multiple_of(s * pw, 128), pw)
    lines = []
    for c in range(C):
        def h_place(q, c=c):
            return heads.at[c, :, pl.ds(pl.multiple_of(q * pw, 128), pw)]

        lines.append(Line(h_place(s), h_place, sh.at[c], rh.at[c]))

    q_iota = lax.broadcasted_iota(jnp.int32, (S * T, 1), 0)
    k_iota = lax.broadcasted_iota(jnp.int32, (1, S * T), 1)

    def attend(c, between):
        for i in range(S):
            mm[i * KQ:(i + 1) * KQ] = (w_all[c, i].astype(jnp.float32) + lax.dot_general(
                a_all[i], b_v[:, wcols(s, c)], (((0,), (0,)), ((), ())), preferred_element_type=jnp.float32)).astype(jnp.bfloat16)
        queries = jnp.dot(xk_all[:, :ql], mm[...], preferred_element_type=jnp.float32)
        qpos = q_iota
        kpos = k_iota
        for i in range(S):
            start = pos_all[i, 0:1, 0:1] - i * T
            qpos = qpos + jnp.where(q_iota // T == i, start, 0)
            kpos = kpos + jnp.where(k_iota // T == i, start, 0)
        visible = kpos <= qpos
        lat = xk_all[:, ql:ql + kvr]
        key_rope = xk_all[:, ql + kvr:ql + kvr + rope]
        contract = (((1,), (1,)), ((), ()))
        for j in range(heads_c):
            qn = queries[:, j * qw:j * qw + nope].astype(jnp.bfloat16)
            qr = queries[:, j * qw + nope:(j + 1) * qw].astype(jnp.bfloat16)
            absorbed = jnp.dot(qn, ku_v[c * heads_c + j], preferred_element_type=jnp.float32).astype(jnp.bfloat16)
            scores = (lax.dot_general(absorbed, lat, contract, preferred_element_type=jnp.float32)
                      + lax.dot_general(qr, key_rope, contract, preferred_element_type=jnp.float32)) * scale
            scores = jnp.where(visible, scores, jnp.float32(-1e30))
            top = jnp.max(scores, axis=1, keepdims=True)
            weights = jnp.where(visible, jnp.exp(scores - top), jnp.float32(0.0))
            row_sum = jnp.sum(weights, axis=1, keepdims=True)
            context = jnp.dot(weights.astype(jnp.bfloat16), lat, preferred_element_type=jnp.float32)
            context = (context / row_sum).astype(jnp.bfloat16)
            res = jnp.dot(context, vu_v[c * heads_c + j], preferred_element_type=jnp.float32).astype(jnp.bfloat16)
            heads[c, :, pl.ds(pl.multiple_of(s * pw + j * vdim, 128), vdim)] = res
            if j == 0:
                between()

    for k in range(1, S):
        q = lax.rem(s - k + S, S)
        gx[k].wait_recv()
        for j in range(1, H):
            to = lax.rem(h + j, H)
            yx[k, j] = go(remote(
                xk_all.at[rows(q), xcols(h)], xk_all.at[rows(q), xcols(h)], sy.at[k, j], ry.at[k, j], head=to))
        ga[k].wait_recv()
        for j in range(1, H):
            to = lax.rem(h + j, H)
            ya[k, j] = go(remote(
                a_all.at[q, arows(h)], a_all.at[q, arows(h)], sb.at[k, j], rb.at[k, j], head=to))
    for cp in own:
        cp.wait()

    def merge_cols(i, carry):
        cols = pl.ds(pl.multiple_of(i * cw, 128), cw)
        m_v[:, cols] = (w_v[:, cols].astype(jnp.float32) + lax.dot_general(
            a_all[s], b_v[:, cols], (((0,), (0,)), ((), ())), preferred_element_type=jnp.float32)).astype(jnp.bfloat16)
        return carry

    lax.fori_loop(0, NC // cw, merge_cols, 0)
    out_m = pltpu.make_async_copy(m_v, merged, loc.at[len(local)])
    out_m.start()
    gv = forward(0)
    for k in range(1, S):
        gp[k].wait_recv()
        for j in range(1, H):
            ya[k, j].wait_recv()
            yx[k, j].wait_recv()
    for c in range(C):
        for k in range(1, S):
            gv[k].wait_recv()
        later = []

        def between():
            if c > 0:
                lines[c - 1].step(1)
            if c < C - 1:
                later.append(forward(c + 1))

        attend(c, between)
        if c < C - 1:
            gv = later[0]
        else:
            lines[c].send()
        if c > 0:
            for d in range(2, S):
                lines[c - 1].step(d)
        if c < C - 1:
            lines[c].send()
    for cp in ops:
        cp.wait()
    nb = 2
    bw = dcols // nb

    def trows(i):
        return pl.ds(pl.multiple_of(i * T, T), T)

    twin, cross = {}, {}

    def reduce_chip(i):
        for x in range(X):
            twin[i, x].wait_recv()
            mid[i, x] = (part[i, trows(2 * x + core)].astype(jnp.float32)
                         + pair[i, x].astype(jnp.float32)).astype(jnp.bfloat16)
        for k in range(1, X):
            x = lax.rem(chip + k, X)
            cross[i, k] = go(remote(mid.at[i, x], got.at[i, k], so.at[i, k], ro.at[i, k], head=2 * x + core))

    for c in range(C):
        for i in range(nb):
            cols = slice(i * bw, (i + 1) * bw)
            if c == C - 1 and i == 0:
                for d in range(2, S):
                    lines[c].step(d)
            acc = jnp.dot(heads[c], op_v[c, :, cols], preferred_element_type=jnp.float32)
            if c > 0:
                acc = acc + total[:, cols]
            if c < C - 1:
                total[:, cols] = acc
                if c == C - 2 and i == 0:
                    lines[C - 1].step(1)
            else:
                part[i] = acc.astype(jnp.bfloat16)
                for x in range(X):
                    twin[i, x] = go(remote(
                        part.at[i, trows(2 * x + 1 - core)], pair.at[i, x], st.at[i, x], rt.at[i, x], head=sibling))
                if i > 0:
                    reduce_chip(i - 1)
    reduce_chip(nb - 1)
    for i in range(nb):
        res = part[i, trows(h)].astype(jnp.float32) + pair[i, chip].astype(jnp.float32)
        for k in range(1, X):
            cross[i, k].wait_recv()
            res = res + got[i, k].astype(jnp.float32)
        mixed[:, i * bw:(i + 1) * bw] = res.astype(jnp.bfloat16)
    for cp in sends:
        cp.wait_send()
    for line in lines:
        line.finish()
    out_m.wait()


def fused(mesh_shape, x, kv, positions, w, a, b, key_up, value_up, out_proj):
    S, H = mesh_shape["seq"], mesh_shape["head"]
    T, ql = x.shape
    KQ, NC = w.shape
    hd, nope, kvr = key_up.shape
    rope = kv.shape[1] - kvr
    vdim = value_up.shape[2]
    hp = hd // S
    heads_c = 2
    C = hp // heads_c
    cw = heads_c * (nope + rope)
    dcols = out_proj.shape[1]
    width = ql + kv.shape[1]
    full = -(-width // (128 * H)) * (128 * H)
    xk = jnp.concatenate([x, kv, jnp.zeros((T, full - width), x.dtype)], axis=1)
    at = jnp.transpose(a)
    scale = 1.0 / math.sqrt(nope + rope)
    dims = (S, H, C, T, KQ, NC, nope, rope, kvr, hp, cw, dcols, scale)
    bf, f32 = jnp.bfloat16, jnp.float32
    dma = pltpu.SemaphoreType.DMA
    nloc = 5 + C + 2 + C * S + 1
    pw = heads_c * vdim
    return pl.pallas_call(
        functools.partial(fused_kernel, dims),
        out_shape=(jax.ShapeDtypeStruct((KQ, NC), bf), jax.ShapeDtypeStruct((T, dcols), bf)),
        in_specs=[pl.BlockSpec(memory_space=pltpu.SMEM)] + [pl.BlockSpec(memory_space=pl.ANY)] * 7,
        out_specs=(pl.BlockSpec(memory_space=pl.ANY), pl.BlockSpec(memory_space=pltpu.VMEM)),
        scratch_shapes=[
            pltpu.VMEM((KQ, NC), bf), pltpu.VMEM((KQ, NC), bf),
            pltpu.VMEM(b.shape, bf), pltpu.VMEM((8, 128), jnp.int32),
            pltpu.VMEM((S * T, full), bf), pltpu.VMEM((S,) + at.shape, bf), pltpu.VMEM((S, 8, 128), jnp.int32),
            pltpu.VMEM((C, S, KQ, cw), bf), pltpu.VMEM((S * KQ, cw), bf),
            pltpu.VMEM((hp, nope, kvr), bf), pltpu.VMEM((hp, kvr, vdim), bf),
            pltpu.VMEM((C, S * pw, dcols), bf), pltpu.VMEM((C, S * T, S * pw), bf), pltpu.VMEM((S * T, dcols), f32),
            pltpu.VMEM((2, S * T, dcols // 2), bf), pltpu.VMEM((2, H // 2, T, dcols // 2), bf),
            pltpu.VMEM((2, H // 2, T, dcols // 2), bf), pltpu.VMEM((2, H // 2, T, dcols // 2), bf),
            dma((nloc,)),
            dma((S,)), dma((S,)), dma((S, H)), dma((S, H)), dma((S,)), dma((S,)), dma((S, H)), dma((S, H)),
            dma((S,)), dma((S,)),
            dma((C, S)), dma((C, S)), dma((C, S)), dma((C, S)), dma((C, 2 * S)), dma((C, S)),
            dma((2, H // 2)), dma((2, H // 2)), dma((2, H // 2)), dma((2, H // 2)),
        ],
        compiler_params=pltpu.CompilerParams(collective_id=0, has_side_effects=True),
    )(positions, w, xk, at, b, key_up, value_up, out_proj)


def fits(shape, x, kv, w, a, key_up, value_up, out_proj):
    S, H = shape["seq"], shape["head"]
    hd, nope, kvr = key_up.shape
    rope = kv.shape[1] - kvr
    return (
        shape["groups"] == 2 and S > 1 and H == S and H % 2 == 0 and hd % (4 * S) == 0
        and (2 * (nope + rope)) % 128 == 0 and w.shape[0] % 32 == 0 and a.shape[1] % (16 * H) == 0 and x.shape[0] % 16 == 0
        and nope % 128 == 0 and kvr % 128 == 0 and value_up.shape[2] % 128 == 0
        and x.shape[1] % 128 == 0 and out_proj.shape[1] % 256 == 0
    )


def on_device(
    query_latent_rows,
    key_value_latents,
    positions,
    query_up_weight,
    adapter_down_factor,
    adapter_up_factor,
    head_key_up_weight,
    head_value_up_weight,
    output_projection_weight,
):
    merged_query_weight = (
        query_up_weight.astype(jnp.float32)
        + jnp.dot(adapter_down_factor, adapter_up_factor, preferred_element_type=jnp.float32)
    ).astype(jnp.bfloat16)
    tok_rows = query_latent_rows.shape[0]
    queries = jnp.dot(
        query_latent_rows,
        lax.all_gather(merged_query_weight, "seq", axis=0, tiled=True),
        preferred_element_type=jnp.float32,
    )
    heads_dev = head_key_up_weight.shape[0]
    nope_dim = head_key_up_weight.shape[1]
    kv_rank = head_key_up_weight.shape[2]
    lat_width = key_value_latents.shape[1]
    score_scale = 1.0 / math.sqrt(nope_dim + lat_width - kv_rank)
    queries = queries.astype(jnp.bfloat16).reshape(tok_rows, heads_dev, -1)
    absorbed = jnp.einsum(
        "thn,hnk->thk",
        queries[:, :, :nope_dim],
        head_key_up_weight,
        preferred_element_type=jnp.float32,
    ).astype(jnp.bfloat16)
    full_query = jnp.concatenate([absorbed, queries[:, :, nope_dim:]], axis=2).reshape(
        tok_rows * heads_dev, lat_width
    )
    query_pos = jnp.repeat(positions, heads_dev)
    q_count = tok_rows * heads_dev
    row_max = jnp.full((q_count,), -1e30, jnp.float32)
    key_rows = lax.all_gather(key_value_latents, "seq", axis=0, tiled=True)
    key_pos = lax.all_gather(positions, "seq", axis=0, tiled=True)
    visible = key_pos[None, :] <= query_pos[:, None]
    scores = (
        lax.dot_general(
            full_query, key_rows, (((1,), (1,)), ((), ())), preferred_element_type=jnp.float32
        )
        * score_scale
    )
    scores = jnp.where(visible, scores, jnp.float32(-1e30))
    new_max = jnp.maximum(row_max, jnp.max(scores, axis=1))
    weights = jnp.where(visible, jnp.exp(scores - new_max[:, None]), jnp.float32(0.0))
    row_sum = jnp.sum(weights, axis=1)
    running = jnp.dot(
        weights.astype(jnp.bfloat16), key_rows[:, :kv_rank], preferred_element_type=jnp.float32
    )
    row_max, row_sum, running = (new_max, row_sum, running)
    context_output = (
        (running / row_sum[:, None]).astype(jnp.bfloat16).reshape(tok_rows, heads_dev, kv_rank)
    )
    heads_out = (
        jnp.einsum(
            "euw,uwz->euz", context_output, head_value_up_weight, preferred_element_type=jnp.float32
        )
        .astype(jnp.bfloat16)
        .reshape(tok_rows, -1)
    )
    partial_value = jnp.dot(
        lax.all_gather(heads_out, "seq", axis=0, tiled=True),
        output_projection_weight,
        preferred_element_type=jnp.float32,
    )
    mixed = lax.psum_scatter(
        partial_value.astype(jnp.bfloat16), "head", scatter_dimension=0, tiled=True
    )
    return (merged_query_weight, mixed)


def solution(mesh):
    placed = (
        P(("groups", "seq"), None),
        P(("groups", "seq"), None),
        P(("groups", "seq")),
        P("seq", "head"),
        P(("groups", "seq"), None),
        P("groups", "head"),
        P("head", None, None),
        P("head", None, None),
        P("head", "seq"),
    )

    def body(x, kv, positions, w, a, b, key_up, value_up, out_proj):
        if fits(mesh.shape, x, kv, w, a, key_up, value_up, out_proj):
            return fused(mesh.shape, x, kv, positions, w, a, b, key_up, value_up, out_proj)
        return on_device(x, kv, positions, w, a, b, key_up, value_up, out_proj)

    return jax.shard_map(
        body,
        mesh=mesh,
        in_specs=placed,
        out_specs=(P(("groups", "seq"), "head"), P(("groups", "head"), "seq")),
        check_vma=False,
    )
```
